128 devices in a mesh: seq: 8 (over z, core), fsdp: 16 (over y, x).
Axes of the slice: x: 4, y: 4, z: 4, core: 2. Of those that a mesh axis runs over, the one named last changes fastest.
Arguments:
- tokens: bfloat16 [2, 16384, 8192], P(None, 'fsdp', 'seq'), may hold values from -6 to 6
- keep_index: int32 [2, 5120], P(None, 'fsdp'), may hold values from 0 to 1024, as said below
- keep_count: int32 [2, 16], replicated, may hold values from 64 to 320, as said below
- block_mask: int32 [2, 16, 16], replicated, may hold values from 0 to 1, as said below
- router: bfloat16 [8192], replicated, may hold values from -0.0625 to 0.0625
- norm_gain: float32 [8192], replicated, may hold values from 0.25 to 1.75
- w_query: bfloat16 [8192, 8192], P('fsdp', 'seq'), may hold values from -3 to 3
- w_key: bfloat16 [8192, 1024], P('fsdp', 'seq'), may hold values from -0.078125 to 0.078125
- w_value: bfloat16 [8192, 1024], P('fsdp', 'seq'), may hold values from -0.0625 to 0.0625
- w_out: bfloat16 [8192, 8192], P('seq', 'fsdp'), may hold values from -0.125 to 0.125
Outputs:
- mixed: float32 [2, 16384, 8192], P(None, 'fsdp', 'seq')
The draws below stay inside these ranges and needn't reach their ends.
Inputs may be any that keep to these rules, and one draw needn't show every extreme that they name: `keep_index`: for each sequence s and fsdp index f, entries f * 320 to f * 320 + keep_count[s, f] - 1 are distinct positions in ascending order, the rest equal 1024. `keep_count`: each count is 64 or 320; the counts of one sequence sum to 2048. `block_mask`: 1 on the diagonal, 0 above it.
All inputs are finite; a program needn't handle non-finite values.
Results may differ from the reference program's by a relative error of at most 0.006.
Values may be sent and summed in bfloat16 or wider, within the bound.
A program may use at most 128 MiB of HBM per device.

```python
import math
import jax
import jax.numpy as jnp
from jax import lax

D = 8192
HQ = 64
KVH = 8
HD = 128
SEQS = 2
LEN = 16384
BLK = 128
KEEP = 2048
TOK_DEV = 1024
KMAX = 320
MASK_BLOCKS = 16
N_SEQ = 8
N_FSDP = 16


def kept_layout(key):
    own_rows = KEEP // N_FSDP
    heavy_count = 5 * own_rows // 2
    light_count = own_rows // 2

    def one_sequence(seq_id):
        seq_key = jax.random.fold_in(key, 1000 + seq_id)
        order = jax.random.permutation(jax.random.fold_in(seq_key, 1), N_FSDP)
        counts = jnp.where(order < N_FSDP // 4, heavy_count, light_count).astype(jnp.int32)

        def one_device(device_id):
            shuffled = jax.random.permutation(jax.random.fold_in(seq_key, 2 + device_id), TOK_DEV)[:KMAX]
            picked = jnp.where(jnp.arange(KMAX) < counts[device_id], shuffled, TOK_DEV)
            return jnp.sort(picked).astype(jnp.int32)
        table = jax.vmap(one_device)(jnp.arange(N_FSDP))
        return (counts, table.reshape(N_FSDP * KMAX))
    return jax.vmap(one_sequence)(jnp.arange(SEQS))


def draw_keep_index(key, part):
    return kept_layout(jax.random.fold_in(key, 7))[1]


def draw_keep_count(key, part):
    return kept_layout(jax.random.fold_in(key, 7))[0]


def draw_block_mask(key, part):
    coin = jax.random.randint(jax.random.fold_in(key, 21), (SEQS, MASK_BLOCKS, MASK_BLOCKS), 0, 2)
    row_ids = jnp.arange(MASK_BLOCKS)[:, None]
    col_ids = jnp.arange(MASK_BLOCKS)[None, :]
    return jnp.where(row_ids == col_ids, 1, jnp.where(col_ids < row_ids, coin, 0)).astype(jnp.int32)


def key_kernel(key):
    values = jax.random.normal(jax.random.fold_in(key, 31), (D, KVH * HD), jnp.float32) * (1.0 / math.sqrt(D))
    return jnp.clip(values, -0.078125, 0.078125)


def draw_w_key(key, part):
    return key_kernel(key).astype(jnp.bfloat16)


def draw_w_query(key, part):
    base = jax.random.normal(jax.random.fold_in(key, 32), (D, HQ * HD), jnp.float32) * (2.0 / math.sqrt(D))
    return jnp.clip(base, -3.0, 3.0).astype(jnp.bfloat16)


def block_scale(own_key, dims, cuts, low, top_value):
    factor_of, own = 1.0, jax.random.fold_in(own_key, 6)
    for dim, shards_of in cuts:
        draws = jnp.exp(jax.random.uniform(jax.random.fold_in(own, dim), (shards_of,), jnp.float32, low / len(cuts), top_value / len(cuts)))
        factor_of = factor_of * jnp.repeat(draws, dims[dim] // shards_of).reshape([-1 if axis == dim else 1 for axis in range(len(dims))])
    return factor_of


def centred(key, extent, spread, limit, shards=(), held_as=jnp.bfloat16):
    values = spread * jax.random.normal(key, extent, jnp.float32)
    if shards:
        values = values * block_scale(key, extent, shards, -0.22, 0.18)
    return jnp.clip(values, -limit, limit).astype(held_as)


def setup_inputs(seed: int = 0) -> dict:
    keys = jax.random.split(jax.random.key(seed), 11)
    return {
        "tokens": centred(keys[0], (SEQS, LEN, D), 1.0, 6.0, ((1, 16), (2, 8))),
        "keep_index": draw_keep_index(jax.random.fold_in(keys[10], 71), 0),
        "keep_count": draw_keep_count(jax.random.fold_in(keys[10], 71), 0),
        "block_mask": draw_block_mask(jax.random.fold_in(keys[10], 71), 0),
        "router": centred(keys[4], (D,), D ** -0.5, 0.0625),
        "norm_gain": jnp.clip(1.0 + 0.15 * jax.random.normal(keys[5], (D,), jnp.float32), 0.25, 1.75),
        "w_query": draw_w_query(jax.random.fold_in(keys[10], 71), 0),
        "w_key": draw_w_key(jax.random.fold_in(keys[10], 71), 0),
        "w_value": centred(keys[8], (D, KVH * HD), D ** -0.5, 0.0625, ((0, 16), (1, 8))),
        "w_out": centred(keys[9], (HQ * HD, D), (HQ * HD // 4) ** -0.5, 0.125, ((0, 8), (1, 16))),
    }


epsilon = 1e-05

def head_attention(operands, allowed):
    query_head, key_head, value_head = operands
    scores = jnp.einsum('gqd,td->gqt', query_head.astype(jnp.float32), key_head.astype(jnp.float32)) * (1.0 / HD ** 0.5)
    scores = jnp.where(allowed[None], scores, jnp.float32(-1e+30))
    row_max = lax.optimization_barrier(jnp.max(scores, axis=2, keepdims=True))
    weights = jnp.where(allowed[None], jnp.exp(scores - row_max), jnp.float32(0.0))
    totals = lax.optimization_barrier(jnp.sum(weights, axis=2, keepdims=True))
    rounded = weights.astype(jnp.bfloat16)
    mixed_values = jnp.einsum('gqt,td->gqd', rounded.astype(jnp.float32), value_head.astype(jnp.float32))
    return (mixed_values / totals).astype(jnp.bfloat16)

def reference(tokens, keep_index, keep_count, block_mask, router, norm_gain, w_query, w_key, w_value, w_out):
    tok_dev = LEN // N_FSDP
    group_size = HQ // KVH
    starts = jnp.cumsum(keep_count, axis=1) - keep_count
    range_ends = starts + keep_count
    kept_rank = jnp.arange(KEEP, dtype=jnp.int32)
    result = tokens.astype(jnp.float32)
    head_width = HQ * HD // N_SEQ
    for seq_id in range(SEQS):
        source = lax.optimization_barrier(jnp.sum((range_ends[seq_id][None, :] <= kept_rank[:, None]).astype(jnp.int32), axis=1)).astype(jnp.int32)
        local_rank = kept_rank - starts[seq_id][source]
        index_table = keep_index[seq_id].reshape(N_FSDP, KMAX)
        position = (source * tok_dev + index_table[source, local_rank]).astype(jnp.int32)
        kept = tokens[seq_id][position]
        router_logit = jnp.dot(kept, router, preferred_element_type=jnp.float32)
        gate_value = jax.nn.sigmoid(router_logit)
        wide = kept.astype(jnp.float32)
        mean_square = lax.optimization_barrier(jnp.mean(wide * wide, axis=1, keepdims=True))
        normed = (wide * lax.rsqrt(mean_square + epsilon) * norm_gain).astype(jnp.bfloat16)
        queries = jnp.dot(normed, w_query, preferred_element_type=jnp.float32).astype(jnp.bfloat16)
        key_rows = jnp.dot(normed, w_key, preferred_element_type=jnp.float32).astype(jnp.bfloat16)
        value_rows = jnp.dot(normed, w_value, preferred_element_type=jnp.float32).astype(jnp.bfloat16)
        block_id = kept_rank // BLK
        open_blocks = block_mask[seq_id][block_id][:, block_id] == 1
        allowed = open_blocks & (kept_rank[None, :] <= kept_rank[:, None])
        query_heads = jnp.transpose(queries.reshape(KEEP, KVH, group_size, HD), (1, 2, 0, 3))
        key_heads = jnp.transpose(key_rows.reshape(KEEP, KVH, HD), (1, 0, 2))
        value_heads = jnp.transpose(value_rows.reshape(KEEP, KVH, HD), (1, 0, 2))
        attended = lax.map(lambda operands: head_attention(operands, allowed), (query_heads, key_heads, value_heads))
        attended = jnp.transpose(attended, (2, 0, 1, 3)).reshape(KEEP, HQ * HD)
        projected = jnp.zeros((KEEP, D), jnp.float32)
        for group_id in range(N_SEQ):
            term = jnp.dot(attended[:, group_id * head_width:(group_id + 1) * head_width], w_out[group_id * head_width:(group_id + 1) * head_width], preferred_element_type=jnp.float32)
            term = lax.optimization_barrier(term.astype(jnp.bfloat16))
            projected = projected + term.astype(jnp.float32)
        update = (gate_value[:, None] * projected).astype(jnp.bfloat16)
        result = result.at[seq_id, position].add(update.astype(jnp.float32))
    return result
```

```python
import math

import jax
import jax.numpy as jnp
from jax import lax
from jax.sharding import PartitionSpec as P

HD = 128
BLK = 128


epsilon = 1e-05


def onehot(index, size):
    return (index[..., None] == jnp.arange(size, dtype=jnp.int32)).astype(jnp.bfloat16)


def select_rows(index, rows):
    picked = jnp.einsum(
        "skp,spc->skc", onehot(index, rows.shape[1]), rows, preferred_element_type=jnp.float32
    )
    return picked.astype(rows.dtype)


def small_take(table, index):
    hits = index[..., None] == jnp.arange(table.shape[1], dtype=jnp.int32)
    return jnp.sum(jnp.where(hits, table[:, None, :], 0), axis=-1)


def gather_all(x, axis_name, count):
    copies = jnp.broadcast_to(x[None], (count,) + x.shape)
    return lax.all_to_all(copies, axis_name, split_axis=0, concat_axis=0, tiled=True)


def shards(
    tokens, keep_index, keep_count, block_mask, router, norm_gain, w_query, w_key, w_value, w_out
):
    fsdp_size = lax.axis_size("fsdp")
    seq_size = lax.axis_size("seq")
    owner_idx = lax.axis_index("fsdp")
    seq_count, tok_dev, part_width = tokens.shape
    kept_most = keep_index.shape[1]
    slot_count = kept_most // fsdp_size
    own_rows = tok_dev // 8
    block_count = block_mask.shape[1]

    in_rows, q_cols = w_query.shape
    kv_cols = w_key.shape[1]
    qkv_local = jnp.concatenate([w_query, w_key, w_value], axis=1)
    packed = jnp.concatenate([qkv_local.reshape(-1), w_out.reshape(-1)])
    gathered = lax.all_gather(packed, "fsdp", axis=0, tiled=False)
    qkv_size = qkv_local.size
    w_qkv = gathered[:, :qkv_size].reshape(fsdp_size * in_rows, q_cols + 2 * kv_cols)
    w_out_blocks = gathered[:, qkv_size:].reshape((fsdp_size,) + w_out.shape)

    starts = jnp.cumsum(keep_count, axis=1) - keep_count
    range_ends = starts + keep_count
    my_start = lax.dynamic_index_in_dim(starts, owner_idx, 1, keepdims=False)
    my_count = lax.dynamic_index_in_dim(keep_count, owner_idx, 1, keepdims=False)

    owner_ids = jnp.arange(fsdp_size, dtype=jnp.int32)[None, :, None]
    slot_ids = jnp.arange(slot_count, dtype=jnp.int32)[None, None, :]
    first_pick = jnp.mod(owner_ids - my_start[:, None, None], fsdp_size)
    pick_index = (first_pick + slot_ids * fsdp_size).reshape(seq_count, -1)
    usable = pick_index < my_count[:, None]
    src_pos = small_take(keep_index, jnp.minimum(pick_index, kept_most - 1))
    src_pos = jnp.where(usable, src_pos, -1)
    send_rows = select_rows(src_pos, tokens).reshape(seq_count, fsdp_size, slot_count, part_width)
    received = lax.all_to_all(send_rows, "fsdp", split_axis=1, concat_axis=1, tiled=True)

    kept_rank = jnp.arange(own_rows, dtype=jnp.int32) * fsdp_size + owner_idx
    source = jnp.sum((range_ends[:, None, :] <= kept_rank[None, :, None]).astype(jnp.int32), axis=2)
    source_start = small_take(starts, source)
    slot_of = (kept_rank[None, :] - source_start) // fsdp_size
    flat_index = source * slot_count + slot_of
    narrow_rows = select_rows(
        flat_index, received.reshape(seq_count, fsdp_size * slot_count, part_width)
    )
    row_parts = gather_all(narrow_rows, "seq", seq_size)
    full_rows = jnp.transpose(row_parts, (1, 2, 0, 3)).reshape(
        seq_count, own_rows, seq_size * part_width
    )
    full_width = full_rows.shape[2]
    row_total = seq_count * own_rows
    flat_rows = full_rows.reshape(row_total, full_width)
    router_logit = jnp.dot(flat_rows, router, preferred_element_type=jnp.float32)
    gate_value = jax.nn.sigmoid(router_logit)
    wide = flat_rows.astype(jnp.float32)
    mean_square = jnp.mean(wide * wide, axis=1, keepdims=True)
    normed = (wide * lax.rsqrt(mean_square + epsilon) * norm_gain).astype(jnp.bfloat16)
    qkv_sum = jnp.dot(normed, w_qkv, preferred_element_type=jnp.float32).astype(jnp.bfloat16)
    local_kv = kv_cols // HD
    local_heads = q_cols // HD
    group_size = local_heads // local_kv
    queries = qkv_sum[:, :q_cols].reshape(seq_count, own_rows, local_kv, group_size, HD)
    kv_rows = qkv_sum[:, q_cols:].reshape(seq_count, own_rows, 2 * kv_cols)
    kv_parts = gather_all(kv_rows, "fsdp", fsdp_size)
    keep_total = fsdp_size * own_rows
    all_kv = jnp.transpose(kv_parts, (1, 0, 2, 3)).reshape(seq_count, keep_total, 2 * kv_cols)
    key_position = jnp.arange(keep_total, dtype=jnp.int32)
    key_rank = key_position % own_rows * fsdp_size + key_position // own_rows
    block_ids = jnp.arange(block_count, dtype=jnp.int32)
    query_onehot = (kept_rank[:, None] // BLK == block_ids[None, :]).astype(jnp.float32)
    key_onehot = (key_rank[:, None] // BLK == block_ids[None, :]).astype(jnp.float32)
    block_open = jnp.einsum(
        "qa,sab,tb->sqt", query_onehot, block_mask.astype(jnp.float32), key_onehot
    )
    allowed = (block_open > 0.5) & (key_rank[None, None, :] <= kept_rank[None, :, None])
    open_mask = allowed[:, None, None, :, :]
    key_heads = all_kv[:, :, :kv_cols].reshape(seq_count, keep_total, local_kv, HD)
    value_heads = all_kv[:, :, kv_cols:].reshape(seq_count, keep_total, local_kv, HD)
    scores = jnp.einsum(
        "sqkgd,stkd->skgqt", queries, key_heads, preferred_element_type=jnp.float32
    ) * (1.0 / math.sqrt(HD))
    scores = jnp.where(open_mask, scores, jnp.float32(-1e30))
    row_max = jnp.max(scores, axis=4, keepdims=True)
    weights = jnp.where(open_mask, jnp.exp(scores - row_max), jnp.float32(0.0))
    totals = jnp.sum(weights, axis=4, keepdims=True)
    mixed_values = jnp.einsum(
        "skgqt,stkd->sqkgd",
        weights.astype(jnp.bfloat16),
        value_heads,
        preferred_element_type=jnp.float32,
    )
    attended = (
        (mixed_values / jnp.transpose(totals, (0, 3, 1, 2, 4)))
        .astype(jnp.bfloat16)
        .reshape(row_total, local_heads * HD)
    )
    partial_value = jnp.einsum(
        "rk,fkc->rfc", attended, w_out_blocks, preferred_element_type=jnp.float32
    )
    summed = lax.psum_scatter(
        partial_value.reshape(seq_count, own_rows, full_width).astype(jnp.bfloat16),
        "seq",
        scatter_dimension=2,
        tiled=True,
    ).astype(jnp.float32)
    update = (gate_value.reshape(seq_count, own_rows, 1) * summed).astype(jnp.bfloat16)

    first_back = jnp.mod(owner_idx - starts, fsdp_size)[:, :, None]
    back_pick = first_back + slot_ids * fsdp_size
    back_usable = (back_pick < keep_count[:, :, None]).reshape(seq_count, -1)
    back_slot = ((starts[:, :, None] + back_pick) // fsdp_size).reshape(seq_count, -1)
    back_slot = jnp.where(back_usable, back_slot, -1)
    back_rows = select_rows(back_slot, update).reshape(
        seq_count, fsdp_size, slot_count, part_width
    )
    returned = lax.all_to_all(back_rows, "fsdp", split_axis=1, concat_axis=1, tiled=True)
    kept_pos = jnp.arange(kept_most, dtype=jnp.int32)
    their_owner = jnp.mod(my_start[:, None] + kept_pos[None, :], fsdp_size)
    flat_back = their_owner * slot_count + kept_pos[None, :] // fsdp_size
    flat_back = jnp.where(kept_pos[None, :] < my_count[:, None], flat_back, -1)
    landed = select_rows(
        flat_back, returned.reshape(seq_count, fsdp_size * slot_count, part_width)
    )
    valid_pos = jnp.where(kept_pos[None, :] < my_count[:, None], keep_index, -1)
    dense_update = jnp.einsum(
        "skp,skc->spc", onehot(valid_pos, tok_dev), landed, preferred_element_type=jnp.float32
    )
    return tokens.astype(jnp.float32) + dense_update


def solution(mesh):
    placed = (
        P(None, "fsdp", "seq"),
        P(None, "fsdp"),
        P(),
        P(),
        P(),
        P(),
        P("fsdp", "seq"),
        P("fsdp", "seq"),
        P("fsdp", "seq"),
        P("seq", "fsdp"),
    )
    return jax.shard_map(
        shards, mesh=mesh, in_specs=placed, out_specs=P(None, "fsdp", "seq"), check_vma=False
    )
```

```python
import math

import jax
import jax.numpy as jnp
from jax import lax
from jax.sharding import PartitionSpec as P

HD = 128
BLK = 128


epsilon = 1e-05


def onehot(index, size):
    return (index[..., None] == jnp.arange(size, dtype=jnp.int32)).astype(jnp.bfloat16)


def select_rows(index, rows):
    picked = jnp.einsum(
        "skp,spc->skc", onehot(index, rows.shape[1]), rows, preferred_element_type=jnp.float32
    )
    return picked.astype(rows.dtype)


def small_take(table, index):
    hits = index[..., None] == jnp.arange(table.shape[1], dtype=jnp.int32)
    return jnp.sum(jnp.where(hits, table[:, None, :], 0), axis=-1)


def gather_all(x, axis_name, count):
    copies = jnp.broadcast_to(x[None], (count,) + x.shape)
    return lax.all_to_all(copies, axis_name, split_axis=0, concat_axis=0, tiled=True)


def shards(
    tokens, keep_index, keep_count, block_mask, router, norm_gain, w_query, w_key, w_value, w_out
):
    fsdp_size = lax.axis_size("fsdp")
    seq_size = lax.axis_size("seq")
    owner_idx = lax.axis_index("fsdp")
    seq_count, tok_dev, part_width = tokens.shape
    kept_most = keep_index.shape[1]
    slot_count = kept_most // fsdp_size
    own_rows = tok_dev // 8
    block_count = block_mask.shape[1]

    in_rows, q_cols = w_query.shape
    kv_cols = w_key.shape[1]
    qkv_cols = q_cols + 2 * kv_cols
    packed = jnp.concatenate([w_query, w_key, w_value, w_out.T], axis=1)
    gathered = lax.all_gather(packed, "fsdp", axis=0, tiled=True)
    w_qkv = gathered[:, :qkv_cols]
    w_out_t = gathered[:, qkv_cols:]

    starts = jnp.cumsum(keep_count, axis=1) - keep_count
    range_ends = starts + keep_count
    my_start = lax.dynamic_index_in_dim(starts, owner_idx, 1, keepdims=False)
    my_count = lax.dynamic_index_in_dim(keep_count, owner_idx, 1, keepdims=False)

    owner_ids = jnp.arange(fsdp_size, dtype=jnp.int32)[None, :, None]
    slot_ids = jnp.arange(slot_count, dtype=jnp.int32)[None, None, :]
    first_pick = jnp.mod(owner_ids - my_start[:, None, None], fsdp_size)
    pick_index = (first_pick + slot_ids * fsdp_size).reshape(seq_count, -1)
    usable = pick_index < my_count[:, None]
    src_pos = small_take(keep_index, jnp.minimum(pick_index, kept_most - 1))
    src_pos = jnp.where(usable, src_pos, -1)
    send_rows = select_rows(src_pos, tokens).reshape(seq_count, fsdp_size, slot_count, part_width)
    received = lax.all_to_all(send_rows, "fsdp", split_axis=1, concat_axis=1, tiled=True)

    kept_rank = jnp.arange(own_rows, dtype=jnp.int32) * fsdp_size + owner_idx
    source = jnp.sum((range_ends[:, None, :] <= kept_rank[None, :, None]).astype(jnp.int32), axis=2)
    source_start = small_take(starts, source)
    slot_of = (kept_rank[None, :] - source_start) // fsdp_size
    flat_index = source * slot_count + slot_of
    narrow_rows = select_rows(
        flat_index, received.reshape(seq_count, fsdp_size * slot_count, part_width)
    )
    row_parts = gather_all(narrow_rows, "seq", seq_size)
    full_rows = jnp.transpose(row_parts, (1, 2, 0, 3)).reshape(
        seq_count, own_rows, seq_size * part_width
    )
    full_width = full_rows.shape[2]
    row_total = seq_count * own_rows
    flat_rows = full_rows.reshape(row_total, full_width)
    router_logit = jnp.dot(flat_rows, router, preferred_element_type=jnp.float32)
    gate_value = jax.nn.sigmoid(router_logit)
    wide = flat_rows.astype(jnp.float32)
    mean_square = jnp.mean(wide * wide, axis=1, keepdims=True)
    normed = (wide * lax.rsqrt(mean_square + epsilon) * norm_gain).astype(jnp.bfloat16)
    qkv_sum = jnp.dot(normed, w_qkv, preferred_element_type=jnp.float32).astype(jnp.bfloat16)
    local_kv = kv_cols // HD
    local_heads = q_cols // HD
    group_size = local_heads // local_kv
    queries = qkv_sum[:, :q_cols].reshape(seq_count, own_rows, local_kv, group_size, HD)
    kv_rows = qkv_sum[:, q_cols:].reshape(seq_count, own_rows, 2 * kv_cols)
    kv_parts = gather_all(kv_rows, "fsdp", fsdp_size)
    keep_total = fsdp_size * own_rows
    all_kv = jnp.transpose(kv_parts, (1, 0, 2, 3)).reshape(seq_count, keep_total, 2 * kv_cols)
    key_position = jnp.arange(keep_total, dtype=jnp.int32)
    key_rank = key_position % own_rows * fsdp_size + key_position // own_rows
    block_ids = jnp.arange(block_count, dtype=jnp.int32)
    query_onehot = (kept_rank[:, None] // BLK == block_ids[None, :]).astype(jnp.float32)
    key_onehot = (key_rank[:, None] // BLK == block_ids[None, :]).astype(jnp.float32)
    block_open = jnp.einsum(
        "qa,sab,tb->sqt", query_onehot, block_mask.astype(jnp.float32), key_onehot
    )
    allowed = (block_open > 0.5) & (key_rank[None, None, :] <= kept_rank[None, :, None])
    open_mask = allowed[:, None, None, :, :]
    key_heads = all_kv[:, :, :kv_cols].reshape(seq_count, keep_total, local_kv, HD)
    value_heads = all_kv[:, :, kv_cols:].reshape(seq_count, keep_total, local_kv, HD)
    scores = jnp.einsum(
        "sqkgd,stkd->skgqt", queries, key_heads, preferred_element_type=jnp.float32
    ) * (1.0 / math.sqrt(HD))
    scores = jnp.where(open_mask, scores, jnp.float32(-1e30))
    row_max = jnp.max(scores, axis=4, keepdims=True)
    weights = jnp.where(open_mask, jnp.exp(scores - row_max), jnp.float32(0.0))
    totals = jnp.sum(weights, axis=4, keepdims=True)
    mixed_values = jnp.einsum(
        "skgqt,stkd->sqkgd",
        weights.astype(jnp.bfloat16),
        value_heads,
        preferred_element_type=jnp.float32,
    )
    attended = (
        (mixed_values / jnp.transpose(totals, (0, 3, 1, 2, 4)))
        .astype(jnp.bfloat16)
        .reshape(row_total, local_heads * HD)
    )
    partial_value = jnp.einsum(
        "rk,nk->rn", attended, w_out_t, preferred_element_type=jnp.float32
    )
    summed = lax.psum_scatter(
        partial_value.reshape(seq_count, own_rows, full_width).astype(jnp.bfloat16),
        "seq",
        scatter_dimension=2,
        tiled=True,
    ).astype(jnp.float32)
    update = (gate_value.reshape(seq_count, own_rows, 1) * summed).astype(jnp.bfloat16)

    first_back = jnp.mod(owner_idx - starts, fsdp_size)[:, :, None]
    back_pick = first_back + slot_ids * fsdp_size
    back_usable = (back_pick < keep_count[:, :, None]).reshape(seq_count, -1)
    back_slot = ((starts[:, :, None] + back_pick) // fsdp_size).reshape(seq_count, -1)
    back_slot = jnp.where(back_usable, back_slot, -1)
    back_rows = select_rows(back_slot, update).reshape(
        seq_count, fsdp_size, slot_count, part_width
    )
    returned = lax.all_to_all(back_rows, "fsdp", split_axis=1, concat_axis=1, tiled=True)
    kept_pos = jnp.arange(kept_most, dtype=jnp.int32)
    their_owner = jnp.mod(my_start[:, None] + kept_pos[None, :], fsdp_size)
    flat_back = their_owner * slot_count + kept_pos[None, :] // fsdp_size
    flat_back = jnp.where(kept_pos[None, :] < my_count[:, None], flat_back, -1)
    landed = select_rows(
        flat_back, returned.reshape(seq_count, fsdp_size * slot_count, part_width)
    )
    valid_pos = jnp.where(kept_pos[None, :] < my_count[:, None], keep_index, -1)
    dense_update = jnp.einsum(
        "skp,skc->spc", onehot(valid_pos, tok_dev), landed, preferred_element_type=jnp.float32
    )
    return tokens.astype(jnp.float32) + dense_update


def solution(mesh):
    placed = (
        P(None, "fsdp", "seq"),
        P(None, "fsdp"),
        P(),
        P(),
        P(),
        P(),
        P("fsdp", "seq"),
        P("fsdp", "seq"),
        P("fsdp", "seq"),
        P("seq", "fsdp"),
    )
    return jax.shard_map(
        shards, mesh=mesh, in_specs=placed, out_specs=P(None, "fsdp", "seq"), check_vma=False
    )
```

```python
import math

import jax
import jax.numpy as jnp
from jax import lax
from jax.sharding import PartitionSpec as P

HD = 128
BLK = 128


epsilon = 1e-05


def onehot(index, size):
    return (index[..., None] == jnp.arange(size, dtype=jnp.int32)).astype(jnp.bfloat16)


def select_rows(index, rows):
    picked = jnp.einsum(
        "skp,spc->skc", onehot(index, rows.shape[1]), rows, preferred_element_type=jnp.float32
    )
    return picked.astype(rows.dtype)


def small_take(table, index):
    hits = index[..., None] == jnp.arange(table.shape[1], dtype=jnp.int32)
    return jnp.sum(jnp.where(hits, table[:, None, :], 0), axis=-1)


def gather_all(x, axis_name, count):
    copies = jnp.broadcast_to(x[None], (count,) + x.shape)
    return lax.all_to_all(copies, axis_name, split_axis=0, concat_axis=0, tiled=True)


def shards(
    tokens, keep_index, keep_count, block_mask, router, norm_gain, w_query, w_key, w_value, w_out
):
    fsdp_size = lax.axis_size("fsdp")
    seq_size = lax.axis_size("seq")
    owner_idx = lax.axis_index("fsdp")
    seq_count, tok_dev, part_width = tokens.shape
    kept_most = keep_index.shape[1]
    slot_count = kept_most // fsdp_size
    own_rows = tok_dev // 8
    block_count = block_mask.shape[1]

    in_rows, q_cols = w_query.shape
    kv_cols = w_key.shape[1]
    qkv_cols = q_cols + 2 * kv_cols
    packed = jnp.concatenate([w_query, w_key, w_value], axis=1)
    w_qkv = lax.all_gather(packed, "fsdp", axis=0, tiled=True)
    w_out_t = lax.all_gather(w_out.T, "fsdp", axis=0, tiled=True)

    starts = jnp.cumsum(keep_count, axis=1) - keep_count
    range_ends = starts + keep_count
    my_start = lax.dynamic_index_in_dim(starts, owner_idx, 1, keepdims=False)
    my_count = lax.dynamic_index_in_dim(keep_count, owner_idx, 1, keepdims=False)

    owner_ids = jnp.arange(fsdp_size, dtype=jnp.int32)[None, :, None]
    slot_ids = jnp.arange(slot_count, dtype=jnp.int32)[None, None, :]
    first_pick = jnp.mod(owner_ids - my_start[:, None, None], fsdp_size)
    pick_index = (first_pick + slot_ids * fsdp_size).reshape(seq_count, -1)
    usable = pick_index < my_count[:, None]
    src_pos = small_take(keep_index, jnp.minimum(pick_index, kept_most - 1))
    src_pos = jnp.where(usable, src_pos, -1)
    send_rows = select_rows(src_pos, tokens).reshape(seq_count, fsdp_size, slot_count, part_width)
    received = lax.all_to_all(send_rows, "fsdp", split_axis=1, concat_axis=1, tiled=True)

    kept_rank = jnp.arange(own_rows, dtype=jnp.int32) * fsdp_size + owner_idx
    source = jnp.sum((range_ends[:, None, :] <= kept_rank[None, :, None]).astype(jnp.int32), axis=2)
    source_start = small_take(starts, source)
    slot_of = (kept_rank[None, :] - source_start) // fsdp_size
    flat_index = source * slot_count + slot_of
    narrow_rows = select_rows(
        flat_index, received.reshape(seq_count, fsdp_size * slot_count, part_width)
    )
    row_parts = gather_all(narrow_rows, "seq", seq_size)
    full_rows = jnp.transpose(row_parts, (1, 2, 0, 3)).reshape(
        seq_count, own_rows, seq_size * part_width
    )
    full_width = full_rows.shape[2]
    row_total = seq_count * own_rows
    flat_rows = full_rows.reshape(row_total, full_width)
    router_logit = jnp.dot(flat_rows, router, preferred_element_type=jnp.float32)
    gate_value = jax.nn.sigmoid(router_logit)
    wide = flat_rows.astype(jnp.float32)
    mean_square = jnp.mean(wide * wide, axis=1, keepdims=True)
    normed = (wide * lax.rsqrt(mean_square + epsilon) * norm_gain).astype(jnp.bfloat16)
    qkv_sum = jnp.dot(normed, w_qkv, preferred_element_type=jnp.float32).astype(jnp.bfloat16)
    local_kv = kv_cols // HD
    local_heads = q_cols // HD
    group_size = local_heads // local_kv
    queries = qkv_sum[:, :q_cols].reshape(seq_count, own_rows, local_kv, group_size, HD)
    kv_rows = qkv_sum[:, q_cols:].reshape(seq_count, own_rows, 2 * kv_cols)
    kv_parts = gather_all(kv_rows, "fsdp", fsdp_size)
    keep_total = fsdp_size * own_rows
    all_kv = jnp.transpose(kv_parts, (1, 0, 2, 3)).reshape(seq_count, keep_total, 2 * kv_cols)
    key_position = jnp.arange(keep_total, dtype=jnp.int32)
    key_rank = key_position % own_rows * fsdp_size + key_position // own_rows
    block_ids = jnp.arange(block_count, dtype=jnp.int32)
    query_onehot = (kept_rank[:, None] // BLK == block_ids[None, :]).astype(jnp.float32)
    key_onehot = (key_rank[:, None] // BLK == block_ids[None, :]).astype(jnp.float32)
    block_open = jnp.einsum(
        "qa,sab,tb->sqt", query_onehot, block_mask.astype(jnp.float32), key_onehot
    )
    allowed = (block_open > 0.5) & (key_rank[None, None, :] <= kept_rank[None, :, None])
    open_mask = allowed[:, None, None, :, :]
    key_heads = all_kv[:, :, :kv_cols].reshape(seq_count, keep_total, local_kv, HD)
    value_heads = all_kv[:, :, kv_cols:].reshape(seq_count, keep_total, local_kv, HD)
    scores = jnp.einsum(
        "sqkgd,stkd->skgqt", queries, key_heads, preferred_element_type=jnp.float32
    ) * (1.0 / math.sqrt(HD))
    scores = jnp.where(open_mask, scores, jnp.float32(-1e30))
    row_max = jnp.max(scores, axis=4, keepdims=True)
    weights = jnp.where(open_mask, jnp.exp(scores - row_max), jnp.float32(0.0))
    totals = jnp.sum(weights, axis=4, keepdims=True)
    mixed_values = jnp.einsum(
        "skgqt,stkd->sqkgd",
        weights.astype(jnp.bfloat16),
        value_heads,
        preferred_element_type=jnp.float32,
    )
    attended = (
        (mixed_values / jnp.transpose(totals, (0, 3, 1, 2, 4)))
        .astype(jnp.bfloat16)
        .reshape(row_total, local_heads * HD)
    )
    partial_value = jnp.einsum(
        "rk,nk->rn", attended, w_out_t, preferred_element_type=jnp.float32
    )
    summed = lax.psum_scatter(
        partial_value.reshape(seq_count, own_rows, full_width).astype(jnp.bfloat16),
        "seq",
        scatter_dimension=2,
        tiled=True,
    ).astype(jnp.float32)
    update = (gate_value.reshape(seq_count, own_rows, 1) * summed).astype(jnp.bfloat16)

    first_back = jnp.mod(owner_idx - starts, fsdp_size)[:, :, None]
    back_pick = first_back + slot_ids * fsdp_size
    back_usable = (back_pick < keep_count[:, :, None]).reshape(seq_count, -1)
    back_slot = ((starts[:, :, None] + back_pick) // fsdp_size).reshape(seq_count, -1)
    back_slot = jnp.where(back_usable, back_slot, -1)
    back_rows = select_rows(back_slot, update).reshape(
        seq_count, fsdp_size, slot_count, part_width
    )
    returned = lax.all_to_all(back_rows, "fsdp", split_axis=1, concat_axis=1, tiled=True)
    kept_pos = jnp.arange(kept_most, dtype=jnp.int32)
    their_owner = jnp.mod(my_start[:, None] + kept_pos[None, :], fsdp_size)
    flat_back = their_owner * slot_count + kept_pos[None, :] // fsdp_size
    flat_back = jnp.where(kept_pos[None, :] < my_count[:, None], flat_back, -1)
    landed = select_rows(
        flat_back, returned.reshape(seq_count, fsdp_size * slot_count, part_width)
    )
    valid_pos = jnp.where(kept_pos[None, :] < my_count[:, None], keep_index, -1)
    dense_update = jnp.einsum(
        "skp,skc->spc", onehot(valid_pos, tok_dev), landed, preferred_element_type=jnp.float32
    )
    return tokens.astype(jnp.float32) + dense_update


def solution(mesh):
    placed = (
        P(None, "fsdp", "seq"),
        P(None, "fsdp"),
        P(),
        P(),
        P(),
        P(),
        P("fsdp", "seq"),
        P("fsdp", "seq"),
        P("fsdp", "seq"),
        P("seq", "fsdp"),
    )
    return jax.shard_map(
        shards, mesh=mesh, in_specs=placed, out_specs=P(None, "fsdp", "seq"), check_vma=False
    )
```

```python
import math

import jax
import jax.numpy as jnp
from jax import lax
from jax.sharding import PartitionSpec as P

HD = 128
BLK = 128


epsilon = 1e-05


def onehot(index, size):
    return (index[..., None] == jnp.arange(size, dtype=jnp.int32)).astype(jnp.bfloat16)


def select_rows(index, rows):
    picked = jnp.einsum(
        "skp,spc->skc", onehot(index, rows.shape[1]), rows, preferred_element_type=jnp.float32
    )
    return picked.astype(rows.dtype)


def small_take(table, index):
    hits = index[..., None] == jnp.arange(table.shape[1], dtype=jnp.int32)
    return jnp.sum(jnp.where(hits, table[:, None, :], 0), axis=-1)


def gather_all(x, axis_name, count):
    copies = jnp.broadcast_to(x[None], (count,) + x.shape)
    return lax.all_to_all(copies, axis_name, split_axis=0, concat_axis=0, tiled=True)


def shards(
    tokens, keep_index, keep_count, block_mask, router, norm_gain, w_query, w_key, w_value, w_out
):
    fsdp_size = lax.axis_size("fsdp")
    seq_size = lax.axis_size("seq")
    owner_idx = lax.axis_index("fsdp")
    seq_count, tok_dev, part_width = tokens.shape
    kept_most = keep_index.shape[1]
    slot_count = kept_most // fsdp_size
    own_rows = tok_dev // 8
    block_count = block_mask.shape[1]

    in_rows, q_cols = w_query.shape
    kv_cols = w_key.shape[1]
    qkv_cols = q_cols + 2 * kv_cols
    w_q_full = lax.all_gather(w_query, "fsdp", axis=0, tiled=True)
    w_kv_full = gather_all(jnp.concatenate([w_key, w_value], axis=1), "fsdp", fsdp_size).reshape(
        fsdp_size * in_rows, 2 * kv_cols
    )
    w_out_t = lax.all_gather(w_out.T, "fsdp", axis=0, tiled=True)

    starts = jnp.cumsum(keep_count, axis=1) - keep_count
    range_ends = starts + keep_count
    my_start = lax.dynamic_index_in_dim(starts, owner_idx, 1, keepdims=False)
    my_count = lax.dynamic_index_in_dim(keep_count, owner_idx, 1, keepdims=False)

    owner_ids = jnp.arange(fsdp_size, dtype=jnp.int32)[None, :, None]
    slot_ids = jnp.arange(slot_count, dtype=jnp.int32)[None, None, :]
    first_pick = jnp.mod(owner_ids - my_start[:, None, None], fsdp_size)
    pick_index = (first_pick + slot_ids * fsdp_size).reshape(seq_count, -1)
    usable = pick_index < my_count[:, None]
    src_pos = small_take(keep_index, jnp.minimum(pick_index, kept_most - 1))
    src_pos = jnp.where(usable, src_pos, -1)
    send_rows = select_rows(src_pos, tokens).reshape(seq_count, fsdp_size, slot_count, part_width)
    received = lax.all_to_all(send_rows, "fsdp", split_axis=1, concat_axis=1, tiled=True)

    kept_rank = jnp.arange(own_rows, dtype=jnp.int32) * fsdp_size + owner_idx
    source = jnp.sum((range_ends[:, None, :] <= kept_rank[None, :, None]).astype(jnp.int32), axis=2)
    source_start = small_take(starts, source)
    slot_of = (kept_rank[None, :] - source_start) // fsdp_size
    flat_index = source * slot_count + slot_of
    narrow_rows = select_rows(
        flat_index, received.reshape(seq_count, fsdp_size * slot_count, part_width)
    )
    row_parts = gather_all(narrow_rows, "seq", seq_size)
    full_rows = jnp.transpose(row_parts, (1, 2, 0, 3)).reshape(
        seq_count, own_rows, seq_size * part_width
    )
    full_width = full_rows.shape[2]
    row_total = seq_count * own_rows
    flat_rows = full_rows.reshape(row_total, full_width)
    router_logit = jnp.dot(flat_rows, router, preferred_element_type=jnp.float32)
    gate_value = jax.nn.sigmoid(router_logit)
    wide = flat_rows.astype(jnp.float32)
    mean_square = jnp.mean(wide * wide, axis=1, keepdims=True)
    normed = (wide * lax.rsqrt(mean_square + epsilon) * norm_gain).astype(jnp.bfloat16)
    q_sum = jnp.dot(normed, w_q_full, preferred_element_type=jnp.float32).astype(jnp.bfloat16)
    kv_sum = jnp.dot(normed, w_kv_full, preferred_element_type=jnp.float32).astype(jnp.bfloat16)
    local_kv = kv_cols // HD
    local_heads = q_cols // HD
    group_size = local_heads // local_kv
    queries = q_sum.reshape(seq_count, own_rows, local_kv, group_size, HD)
    kv_rows = kv_sum.reshape(seq_count, own_rows, 2 * kv_cols)
    kv_parts = gather_all(kv_rows, "fsdp", fsdp_size)
    keep_total = fsdp_size * own_rows
    all_kv = jnp.transpose(kv_parts, (1, 0, 2, 3)).reshape(seq_count, keep_total, 2 * kv_cols)
    key_position = jnp.arange(keep_total, dtype=jnp.int32)
    key_rank = key_position % own_rows * fsdp_size + key_position // own_rows
    block_ids = jnp.arange(block_count, dtype=jnp.int32)
    query_onehot = (kept_rank[:, None] // BLK == block_ids[None, :]).astype(jnp.float32)
    key_onehot = (key_rank[:, None] // BLK == block_ids[None, :]).astype(jnp.float32)
    block_open = jnp.einsum(
        "qa,sab,tb->sqt", query_onehot, block_mask.astype(jnp.float32), key_onehot
    )
    allowed = (block_open > 0.5) & (key_rank[None, None, :] <= kept_rank[None, :, None])
    open_mask = allowed[:, None, None, :, :]
    key_heads = all_kv[:, :, :kv_cols].reshape(seq_count, keep_total, local_kv, HD)
    value_heads = all_kv[:, :, kv_cols:].reshape(seq_count, keep_total, local_kv, HD)
    scores = jnp.einsum(
        "sqkgd,stkd->skgqt", queries, key_heads, preferred_element_type=jnp.float32
    ) * (1.0 / math.sqrt(HD))
    scores = jnp.where(open_mask, scores, jnp.float32(-1e30))
    row_max = jnp.max(scores, axis=4, keepdims=True)
    weights = jnp.where(open_mask, jnp.exp(scores - row_max), jnp.float32(0.0))
    totals = jnp.sum(weights, axis=4, keepdims=True)
    mixed_values = jnp.einsum(
        "skgqt,stkd->sqkgd",
        weights.astype(jnp.bfloat16),
        value_heads,
        preferred_element_type=jnp.float32,
    )
    attended = (
        (mixed_values / jnp.transpose(totals, (0, 3, 1, 2, 4)))
        .astype(jnp.bfloat16)
        .reshape(row_total, local_heads * HD)
    )
    partial_value = jnp.einsum(
        "rk,nk->rn", attended, w_out_t, preferred_element_type=jnp.float32
    )
    summed = lax.psum_scatter(
        partial_value.reshape(seq_count, own_rows, full_width).astype(jnp.bfloat16),
        "seq",
        scatter_dimension=2,
        tiled=True,
    ).astype(jnp.float32)
    update = (gate_value.reshape(seq_count, own_rows, 1) * summed).astype(jnp.bfloat16)

    first_back = jnp.mod(owner_idx - starts, fsdp_size)[:, :, None]
    back_pick = first_back + slot_ids * fsdp_size
    back_usable = (back_pick < keep_count[:, :, None]).reshape(seq_count, -1)
    back_slot = ((starts[:, :, None] + back_pick) // fsdp_size).reshape(seq_count, -1)
    back_slot = jnp.where(back_usable, back_slot, -1)
    back_rows = select_rows(back_slot, update).reshape(
        seq_count, fsdp_size, slot_count, part_width
    )
    returned = lax.all_to_all(back_rows, "fsdp", split_axis=1, concat_axis=1, tiled=True)
    kept_pos = jnp.arange(kept_most, dtype=jnp.int32)
    their_owner = jnp.mod(my_start[:, None] + kept_pos[None, :], fsdp_size)
    flat_back = their_owner * slot_count + kept_pos[None, :] // fsdp_size
    flat_back = jnp.where(kept_pos[None, :] < my_count[:, None], flat_back, -1)
    landed = select_rows(
        flat_back, returned.reshape(seq_count, fsdp_size * slot_count, part_width)
    )
    valid_pos = jnp.where(kept_pos[None, :] < my_count[:, None], keep_index, -1)
    dense_update = jnp.einsum(
        "skp,skc->spc", onehot(valid_pos, tok_dev), landed, preferred_element_type=jnp.float32
    )
    return tokens.astype(jnp.float32) + dense_update


def solution(mesh):
    placed = (
        P(None, "fsdp", "seq"),
        P(None, "fsdp"),
        P(),
        P(),
        P(),
        P(),
        P("fsdp", "seq"),
        P("fsdp", "seq"),
        P("fsdp", "seq"),
        P("seq", "fsdp"),
    )
    return jax.shard_map(
        shards, mesh=mesh, in_specs=placed, out_specs=P(None, "fsdp", "seq"), check_vma=False
    )
```

```python
import math

import jax
import jax.numpy as jnp
from jax import lax
from jax.sharding import PartitionSpec as P

HD = 128
BLK = 128


epsilon = 1e-05


def onehot(index, size):
    return (index[..., None] == jnp.arange(size, dtype=jnp.int32)).astype(jnp.bfloat16)


def select_rows(index, rows):
    picked = jnp.einsum(
        "skp,spc->skc", onehot(index, rows.shape[1]), rows, preferred_element_type=jnp.float32
    )
    return picked.astype(rows.dtype)


def small_take(table, index):
    hits = index[..., None] == jnp.arange(table.shape[1], dtype=jnp.int32)
    return jnp.sum(jnp.where(hits, table[:, None, :], 0), axis=-1)


def gather_all(x, axis_name, count):
    copies = jnp.broadcast_to(x[None], (count,) + x.shape)
    return lax.all_to_all(copies, axis_name, split_axis=0, concat_axis=0, tiled=True)


def shards(
    tokens, keep_index, keep_count, block_mask, router, norm_gain, w_query, w_key, w_value, w_out
):
    fsdp_size = lax.axis_size("fsdp")
    seq_size = lax.axis_size("seq")
    owner_idx = lax.axis_index("fsdp")
    seq_count, tok_dev, part_width = tokens.shape
    kept_most = keep_index.shape[1]
    slot_count = kept_most // fsdp_size
    own_rows = tok_dev // 8
    block_count = block_mask.shape[1]

    in_rows, q_cols = w_query.shape
    kv_cols = w_key.shape[1]
    qkv_cols = q_cols + 2 * kv_cols
    packed = jnp.concatenate([w_query, w_key, w_value], axis=1)
    w_qkv = lax.all_gather(packed, "fsdp", axis=0, tiled=True)
    w_out_t = lax.all_gather(w_out.T, "fsdp", axis=0, tiled=True)

    starts = jnp.cumsum(keep_count, axis=1) - keep_count
    range_ends = starts + keep_count
    my_start = lax.dynamic_index_in_dim(starts, owner_idx, 1, keepdims=False)
    my_count = lax.dynamic_index_in_dim(keep_count, owner_idx, 1, keepdims=False)

    owner_ids = jnp.arange(fsdp_size, dtype=jnp.int32)[None, :, None]
    slot_ids = jnp.arange(slot_count, dtype=jnp.int32)[None, None, :]
    first_pick = jnp.mod(owner_ids - my_start[:, None, None], fsdp_size)
    pick_index = (first_pick + slot_ids * fsdp_size).reshape(seq_count, -1)
    usable = pick_index < my_count[:, None]
    src_pos = small_take(keep_index, jnp.minimum(pick_index, kept_most - 1))
    src_pos = jnp.where(usable, src_pos, -1)
    send_rows = select_rows(src_pos, tokens).reshape(seq_count, fsdp_size, slot_count, part_width)
    received = lax.all_to_all(send_rows, "fsdp", split_axis=1, concat_axis=1, tiled=True)

    kept_rank = jnp.arange(own_rows, dtype=jnp.int32) * fsdp_size + owner_idx
    source = jnp.sum((range_ends[:, None, :] <= kept_rank[None, :, None]).astype(jnp.int32), axis=2)
    source_start = small_take(starts, source)
    slot_of = (kept_rank[None, :] - source_start) // fsdp_size
    flat_index = source * slot_count + slot_of
    narrow_rows = select_rows(
        flat_index, received.reshape(seq_count, fsdp_size * slot_count, part_width)
    )
    row_parts = gather_all(narrow_rows, "seq", seq_size)
    full_rows = jnp.transpose(row_parts, (1, 2, 0, 3)).reshape(
        seq_count, own_rows, seq_size * part_width
    )
    full_width = full_rows.shape[2]
    row_total = seq_count * own_rows
    flat_rows = full_rows.reshape(row_total, full_width)
    router_logit = jnp.dot(flat_rows, router, preferred_element_type=jnp.float32)
    gate_value = jax.nn.sigmoid(router_logit)
    wide = flat_rows.astype(jnp.float32)
    mean_square = jnp.mean(wide * wide, axis=1, keepdims=True)
    normed = (wide * lax.rsqrt(mean_square + epsilon) * norm_gain).astype(jnp.bfloat16)
    qkv_sum = jnp.dot(normed, w_qkv, preferred_element_type=jnp.float32).astype(jnp.bfloat16)
    local_kv = kv_cols // HD
    local_heads = q_cols // HD
    group_size = local_heads // local_kv
    queries = qkv_sum[:, :q_cols].reshape(seq_count, own_rows, local_kv, group_size, HD)
    kv_rows = qkv_sum[:, q_cols:].reshape(seq_count, own_rows, 2 * kv_cols)
    kv_parts = gather_all(kv_rows, "fsdp", fsdp_size)
    keep_total = fsdp_size * own_rows
    all_kv = jnp.transpose(kv_parts, (1, 0, 2, 3)).reshape(seq_count, keep_total, 2 * kv_cols)
    key_position = jnp.arange(keep_total, dtype=jnp.int32)
    key_rank = key_position % own_rows * fsdp_size + key_position // own_rows
    block_ids = jnp.arange(block_count, dtype=jnp.int32)
    query_onehot = (kept_rank[:, None] // BLK == block_ids[None, :]).astype(jnp.float32)
    key_onehot = (key_rank[:, None] // BLK == block_ids[None, :]).astype(jnp.float32)
    block_open = jnp.einsum(
        "qa,sab,tb->sqt", query_onehot, block_mask.astype(jnp.float32), key_onehot
    )
    allowed = (block_open > 0.5) & (key_rank[None, None, :] <= kept_rank[None, :, None])
    open_mask = allowed[:, None, None, :, :]
    key_heads = all_kv[:, :, :kv_cols].reshape(seq_count, keep_total, local_kv, HD)
    value_heads = all_kv[:, :, kv_cols:].reshape(seq_count, keep_total, local_kv, HD)
    scores = jnp.einsum(
        "sqkgd,stkd->skgqt", queries, key_heads, preferred_element_type=jnp.float32
    ) * (1.0 / math.sqrt(HD))
    scores = jnp.where(open_mask, scores, jnp.float32(-1e30))
    row_max = jnp.max(scores, axis=4, keepdims=True)
    weights = jnp.where(open_mask, jnp.exp(scores - row_max), jnp.float32(0.0))
    totals = jnp.sum(weights, axis=4, keepdims=True)
    mixed_values = jnp.einsum(
        "skgqt,stkd->sqkgd",
        weights.astype(jnp.bfloat16),
        value_heads,
        preferred_element_type=jnp.float32,
    )
    attended = (
        (mixed_values / jnp.transpose(totals, (0, 3, 1, 2, 4)))
        .astype(jnp.bfloat16)
        .reshape(row_total, local_heads * HD)
    )
    partial_value = jnp.einsum(
        "rk,jck->jrc",
        attended,
        w_out_t.reshape(seq_size, part_width, local_heads * HD),
        preferred_element_type=jnp.float32,
    )
    summed = lax.psum_scatter(
        partial_value.astype(jnp.bfloat16), "seq", scatter_dimension=0, tiled=True
    ).reshape(seq_count, own_rows, part_width).astype(jnp.float32)
    update = (gate_value.reshape(seq_count, own_rows, 1) * summed).astype(jnp.bfloat16)

    first_back = jnp.mod(owner_idx - starts, fsdp_size)[:, :, None]
    back_pick = first_back + slot_ids * fsdp_size
    back_usable = (back_pick < keep_count[:, :, None]).reshape(seq_count, -1)
    back_slot = ((starts[:, :, None] + back_pick) // fsdp_size).reshape(seq_count, -1)
    back_slot = jnp.where(back_usable, back_slot, -1)
    back_rows = select_rows(back_slot, update).reshape(
        seq_count, fsdp_size, slot_count, part_width
    )
    returned = lax.all_to_all(back_rows, "fsdp", split_axis=1, concat_axis=1, tiled=True)
    kept_pos = jnp.arange(kept_most, dtype=jnp.int32)
    their_owner = jnp.mod(my_start[:, None] + kept_pos[None, :], fsdp_size)
    flat_back = their_owner * slot_count + kept_pos[None, :] // fsdp_size
    flat_back = jnp.where(kept_pos[None, :] < my_count[:, None], flat_back, -1)
    landed = select_rows(
        flat_back, returned.reshape(seq_count, fsdp_size * slot_count, part_width)
    )
    valid_pos = jnp.where(kept_pos[None, :] < my_count[:, None], keep_index, -1)
    dense_update = jnp.einsum(
        "skp,skc->spc", onehot(valid_pos, tok_dev), landed, preferred_element_type=jnp.float32
    )
    return tokens.astype(jnp.float32) + dense_update


def solution(mesh):
    placed = (
        P(None, "fsdp", "seq"),
        P(None, "fsdp"),
        P(),
        P(),
        P(),
        P(),
        P("fsdp", "seq"),
        P("fsdp", "seq"),
        P("fsdp", "seq"),
        P("seq", "fsdp"),
    )
    return jax.shard_map(
        shards, mesh=mesh, in_specs=placed, out_specs=P(None, "fsdp", "seq"), check_vma=False
    )
```

```python
import math

import jax
import jax.numpy as jnp
from jax import lax
from jax.sharding import PartitionSpec as P

HD = 128
BLK = 128


epsilon = 1e-05


def onehot(index, size):
    return (index[..., None] == jnp.arange(size, dtype=jnp.int32)).astype(jnp.bfloat16)


def select_rows(index, rows):
    picked = jnp.einsum(
        "skp,spc->skc", onehot(index, rows.shape[1]), rows, preferred_element_type=jnp.float32
    )
    return picked.astype(rows.dtype)


def small_take(table, index):
    hits = index[..., None] == jnp.arange(table.shape[1], dtype=jnp.int32)
    return jnp.sum(jnp.where(hits, table[:, None, :], 0), axis=-1)


def gather_all(x, axis_name, count):
    copies = jnp.broadcast_to(x[None], (count,) + x.shape)
    return lax.all_to_all(copies, axis_name, split_axis=0, concat_axis=0, tiled=True)


def shards(
    tokens, keep_index, keep_count, block_mask, router, norm_gain, w_query, w_key, w_value, w_out
):
    fsdp_size = lax.axis_size("fsdp")
    seq_size = lax.axis_size("seq")
    owner_idx = lax.axis_index("fsdp")
    seq_count, tok_dev, part_width = tokens.shape
    kept_most = keep_index.shape[1]
    slot_count = kept_most // fsdp_size
    own_rows = tok_dev // 8
    block_count = block_mask.shape[1]

    in_rows, q_cols = w_query.shape
    kv_cols = w_key.shape[1]
    qkv_cols = q_cols + 2 * kv_cols
    packed = jnp.concatenate([w_query, w_key, w_value], axis=1)
    w_qkv = lax.all_gather(packed, "fsdp", axis=0, tiled=True)
    w_out_t = lax.all_gather(w_out.T, "fsdp", axis=0, tiled=True)

    starts = jnp.cumsum(keep_count, axis=1) - keep_count
    range_ends = starts + keep_count
    my_start = lax.dynamic_index_in_dim(starts, owner_idx, 1, keepdims=False)
    my_count = lax.dynamic_index_in_dim(keep_count, owner_idx, 1, keepdims=False)

    owner_ids = jnp.arange(fsdp_size, dtype=jnp.int32)[None, :, None]
    slot_ids = jnp.arange(slot_count, dtype=jnp.int32)[None, None, :]
    first_pick = jnp.mod(owner_ids - my_start[:, None, None], fsdp_size)
    pick_index = (first_pick + slot_ids * fsdp_size).reshape(seq_count, -1)
    usable = pick_index < my_count[:, None]
    src_pos = small_take(keep_index, jnp.minimum(pick_index, kept_most - 1))
    src_pos = jnp.where(usable, src_pos, -1)
    send_rows = select_rows(src_pos, tokens).reshape(seq_count, fsdp_size, slot_count, part_width)
    received = lax.all_to_all(send_rows, "fsdp", split_axis=1, concat_axis=1, tiled=True)

    kept_rank = jnp.arange(own_rows, dtype=jnp.int32) * fsdp_size + owner_idx
    source = jnp.sum((range_ends[:, None, :] <= kept_rank[None, :, None]).astype(jnp.int32), axis=2)
    source_start = small_take(starts, source)
    slot_of = (kept_rank[None, :] - source_start) // fsdp_size
    flat_index = source * slot_count + slot_of
    narrow_rows = select_rows(
        flat_index, received.reshape(seq_count, fsdp_size * slot_count, part_width)
    )
    row_total = seq_count * own_rows
    full_width = seq_size * part_width
    row_parts = gather_all(narrow_rows.reshape(row_total, part_width), "seq", seq_size)
    router_logit = jnp.einsum(
        "jrc,jc->r", row_parts, router.reshape(seq_size, part_width),
        preferred_element_type=jnp.float32,
    )
    gate_value = jax.nn.sigmoid(router_logit)
    wide = row_parts.astype(jnp.float32)
    mean_square = jnp.sum(wide * wide, axis=(0, 2)) / full_width
    normed = (
        wide
        * lax.rsqrt(mean_square + epsilon)[None, :, None]
        * norm_gain.reshape(seq_size, 1, part_width)
    ).astype(jnp.bfloat16)
    qkv_sum = jnp.einsum(
        "jrc,jcn->rn", normed, w_qkv.reshape(seq_size, part_width, qkv_cols),
        preferred_element_type=jnp.float32,
    ).astype(jnp.bfloat16)
    local_kv = kv_cols // HD
    local_heads = q_cols // HD
    group_size = local_heads // local_kv
    queries = qkv_sum[:, :q_cols].reshape(seq_count, own_rows, local_kv, group_size, HD)
    kv_rows = qkv_sum[:, q_cols:].reshape(seq_count, own_rows, 2 * kv_cols)
    kv_parts = gather_all(kv_rows, "fsdp", fsdp_size)
    keep_total = fsdp_size * own_rows
    all_kv = jnp.transpose(kv_parts, (1, 0, 2, 3)).reshape(seq_count, keep_total, 2 * kv_cols)
    key_position = jnp.arange(keep_total, dtype=jnp.int32)
    key_rank = key_position % own_rows * fsdp_size + key_position // own_rows
    block_ids = jnp.arange(block_count, dtype=jnp.int32)
    query_onehot = (kept_rank[:, None] // BLK == block_ids[None, :]).astype(jnp.float32)
    key_onehot = (key_rank[:, None] // BLK == block_ids[None, :]).astype(jnp.float32)
    block_open = jnp.einsum(
        "qa,sab,tb->sqt", query_onehot, block_mask.astype(jnp.float32), key_onehot
    )
    allowed = (block_open > 0.5) & (key_rank[None, None, :] <= kept_rank[None, :, None])
    open_mask = allowed[:, None, None, :, :]
    key_heads = all_kv[:, :, :kv_cols].reshape(seq_count, keep_total, local_kv, HD)
    value_heads = all_kv[:, :, kv_cols:].reshape(seq_count, keep_total, local_kv, HD)
    scores = jnp.einsum(
        "sqkgd,stkd->skgqt", queries, key_heads, preferred_element_type=jnp.float32
    ) * (1.0 / math.sqrt(HD))
    scores = jnp.where(open_mask, scores, jnp.float32(-1e30))
    row_max = jnp.max(scores, axis=4, keepdims=True)
    weights = jnp.where(open_mask, jnp.exp(scores - row_max), jnp.float32(0.0))
    totals = jnp.sum(weights, axis=4, keepdims=True)
    mixed_values = jnp.einsum(
        "skgqt,stkd->sqkgd",
        weights.astype(jnp.bfloat16),
        value_heads,
        preferred_element_type=jnp.float32,
    )
    attended = (
        (mixed_values / jnp.transpose(totals, (0, 3, 1, 2, 4)))
        .astype(jnp.bfloat16)
        .reshape(row_total, local_heads * HD)
    )
    partial_value = jnp.einsum(
        "rk,nk->rn", attended, w_out_t, preferred_element_type=jnp.float32
    )
    summed = lax.psum_scatter(
        partial_value.reshape(seq_count, own_rows, full_width).astype(jnp.bfloat16),
        "seq",
        scatter_dimension=2,
        tiled=True,
    ).astype(jnp.float32)
    update = (gate_value.reshape(seq_count, own_rows, 1) * summed).astype(jnp.bfloat16)

    first_back = jnp.mod(owner_idx - starts, fsdp_size)[:, :, None]
    back_pick = first_back + slot_ids * fsdp_size
    back_usable = (back_pick < keep_count[:, :, None]).reshape(seq_count, -1)
    back_slot = ((starts[:, :, None] + back_pick) // fsdp_size).reshape(seq_count, -1)
    back_slot = jnp.where(back_usable, back_slot, -1)
    back_rows = select_rows(back_slot, update).reshape(
        seq_count, fsdp_size, slot_count, part_width
    )
    returned = lax.all_to_all(back_rows, "fsdp", split_axis=1, concat_axis=1, tiled=True)
    kept_pos = jnp.arange(kept_most, dtype=jnp.int32)
    their_owner = jnp.mod(my_start[:, None] + kept_pos[None, :], fsdp_size)
    flat_back = their_owner * slot_count + kept_pos[None, :] // fsdp_size
    flat_back = jnp.where(kept_pos[None, :] < my_count[:, None], flat_back, -1)
    landed = select_rows(
        flat_back, returned.reshape(seq_count, fsdp_size * slot_count, part_width)
    )
    valid_pos = jnp.where(kept_pos[None, :] < my_count[:, None], keep_index, -1)
    dense_update = jnp.einsum(
        "skp,skc->spc", onehot(valid_pos, tok_dev), landed, preferred_element_type=jnp.float32
    )
    return tokens.astype(jnp.float32) + dense_update


def solution(mesh):
    placed = (
        P(None, "fsdp", "seq"),
        P(None, "fsdp"),
        P(),
        P(),
        P(),
        P(),
        P("fsdp", "seq"),
        P("fsdp", "seq"),
        P("fsdp", "seq"),
        P("seq", "fsdp"),
    )
    return jax.shard_map(
        shards, mesh=mesh, in_specs=placed, out_specs=P(None, "fsdp", "seq"), check_vma=False
    )
```

```python
import math

import jax
import jax.numpy as jnp
from jax import lax
from jax.sharding import PartitionSpec as P

HD = 128
BLK = 128


epsilon = 1e-05


def onehot(index, size):
    return (index[..., None] == jnp.arange(size, dtype=jnp.int32)).astype(jnp.bfloat16)


def select_rows(index, rows):
    picked = jnp.einsum(
        "skp,spc->skc", onehot(index, rows.shape[1]), rows, preferred_element_type=jnp.float32
    )
    return picked.astype(rows.dtype)


def small_take(table, index):
    hits = index[..., None] == jnp.arange(table.shape[1], dtype=jnp.int32)
    return jnp.sum(jnp.where(hits, table[:, None, :], 0), axis=-1)


def gather_all(x, axis_name, count):
    copies = jnp.broadcast_to(x[None], (count,) + x.shape)
    return lax.all_to_all(copies, axis_name, split_axis=0, concat_axis=0, tiled=True)


def shards(
    tokens, keep_index, keep_count, block_mask, router, norm_gain, w_query, w_key, w_value, w_out
):
    fsdp_size = lax.axis_size("fsdp")
    seq_size = lax.axis_size("seq")
    owner_idx = lax.axis_index("fsdp")
    seq_count, tok_dev, part_width = tokens.shape
    kept_most = keep_index.shape[1]
    slot_count = kept_most // fsdp_size
    own_rows = tok_dev // 8
    block_count = block_mask.shape[1]

    in_rows, q_cols = w_query.shape
    kv_cols = w_key.shape[1]
    qkv_cols = q_cols + 2 * kv_cols
    packed = jnp.concatenate([w_query, w_key, w_value], axis=1)
    w_qkv = lax.all_gather(packed, "fsdp", axis=0, tiled=True)
    w_out_t = lax.all_gather(w_out.T, "fsdp", axis=0, tiled=True)

    starts = jnp.cumsum(keep_count, axis=1) - keep_count
    range_ends = starts + keep_count
    my_start = lax.dynamic_index_in_dim(starts, owner_idx, 1, keepdims=False)
    my_count = lax.dynamic_index_in_dim(keep_count, owner_idx, 1, keepdims=False)

    owner_ids = jnp.arange(fsdp_size, dtype=jnp.int32)[None, :, None]
    slot_ids = jnp.arange(slot_count, dtype=jnp.int32)[None, None, :]
    first_pick = jnp.mod(owner_ids - my_start[:, None, None], fsdp_size)
    pick_index = (first_pick + slot_ids * fsdp_size).reshape(seq_count, -1)
    usable = pick_index < my_count[:, None]
    src_pos = small_take(keep_index, jnp.minimum(pick_index, kept_most - 1))
    src_pos = jnp.where(usable, src_pos, -1)
    send_rows = select_rows(src_pos, tokens).reshape(seq_count, fsdp_size, slot_count, part_width)
    received = lax.all_to_all(send_rows, "fsdp", split_axis=1, concat_axis=1, tiled=True)

    kept_rank = jnp.arange(own_rows, dtype=jnp.int32) * fsdp_size + owner_idx
    source = jnp.sum((range_ends[:, None, :] <= kept_rank[None, :, None]).astype(jnp.int32), axis=2)
    source_start = small_take(starts, source)
    slot_of = (kept_rank[None, :] - source_start) // fsdp_size
    flat_index = source * slot_count + slot_of
    narrow_rows = select_rows(
        flat_index, received.reshape(seq_count, fsdp_size * slot_count, part_width)
    )
    row_parts = gather_all(narrow_rows, "seq", seq_size)
    full_rows = jnp.transpose(row_parts, (1, 2, 0, 3)).reshape(
        seq_count, own_rows, seq_size * part_width
    )
    full_width = full_rows.shape[2]
    row_total = seq_count * own_rows
    flat_rows = full_rows.reshape(row_total, full_width)
    router_logit = jnp.dot(flat_rows, router, preferred_element_type=jnp.float32)
    gate_value = jax.nn.sigmoid(router_logit)
    wide = flat_rows.astype(jnp.float32)
    mean_square = jnp.mean(wide * wide, axis=1, keepdims=True)
    normed = (wide * lax.rsqrt(mean_square + epsilon) * norm_gain).astype(jnp.bfloat16)
    qkv_sum = jnp.dot(normed, w_qkv, preferred_element_type=jnp.float32).astype(jnp.bfloat16)
    local_kv = kv_cols // HD
    local_heads = q_cols // HD
    group_size = local_heads // local_kv
    queries = qkv_sum[:, :q_cols].reshape(seq_count, own_rows, local_kv, group_size, HD)
    kv_rows = qkv_sum[:, q_cols:].reshape(seq_count, own_rows, 2 * kv_cols)
    kv_parts = gather_all(kv_rows, "fsdp", fsdp_size)
    keep_total = fsdp_size * own_rows
    all_kv = jnp.transpose(kv_parts, (1, 0, 2, 3)).reshape(seq_count, keep_total, 2 * kv_cols)
    key_position = jnp.arange(keep_total, dtype=jnp.int32)
    key_rank = key_position % own_rows * fsdp_size + key_position // own_rows
    block_ids = jnp.arange(block_count, dtype=jnp.int32)
    query_onehot = (kept_rank[:, None] // BLK == block_ids[None, :]).astype(jnp.float32)
    key_onehot = (key_rank[:, None] // BLK == block_ids[None, :]).astype(jnp.float32)
    block_open = jnp.einsum(
        "qa,sab,tb->sqt", query_onehot, block_mask.astype(jnp.float32), key_onehot
    )
    allowed = (block_open > 0.5) & (key_rank[None, None, :] <= kept_rank[None, :, None])
    open_mask = allowed[:, None, None, :, :]
    key_heads = all_kv[:, :, :kv_cols].reshape(seq_count, keep_total, local_kv, HD)
    value_heads = all_kv[:, :, kv_cols:].reshape(seq_count, keep_total, local_kv, HD)
    scores = jnp.einsum(
        "sqkgd,stkd->skgqt", queries, key_heads, preferred_element_type=jnp.float32
    ) * (1.0 / math.sqrt(HD))
    scores = jnp.where(open_mask, scores, jnp.float32(-1e30))
    row_max = jnp.max(scores, axis=4, keepdims=True)
    weights = jnp.where(open_mask, jnp.exp(scores - row_max), jnp.float32(0.0))
    totals = jnp.sum(weights, axis=4, keepdims=True)
    mixed_values = jnp.einsum(
        "skgqt,stkd->sqkgd",
        weights.astype(jnp.bfloat16),
        value_heads,
        preferred_element_type=jnp.float32,
    )
    attended = (
        (mixed_values / jnp.transpose(totals, (0, 3, 1, 2, 4)))
        .astype(jnp.bfloat16)
        .reshape(row_total, local_heads * HD)
    )
    partial_value = jnp.einsum(
        "rk,nk->rn", attended, w_out_t, preferred_element_type=jnp.float32
    )
    terms = lax.all_to_all(
        partial_value.astype(jnp.bfloat16).reshape(row_total, seq_size, part_width),
        "seq", split_axis=1, concat_axis=1, tiled=True,
    )
    summed = jnp.sum(terms.astype(jnp.float32), axis=1).reshape(seq_count, own_rows, part_width)
    update = (gate_value.reshape(seq_count, own_rows, 1) * summed).astype(jnp.bfloat16)

    first_back = jnp.mod(owner_idx - starts, fsdp_size)[:, :, None]
    back_pick = first_back + slot_ids * fsdp_size
    back_usable = (back_pick < keep_count[:, :, None]).reshape(seq_count, -1)
    back_slot = ((starts[:, :, None] + back_pick) // fsdp_size).reshape(seq_count, -1)
    back_slot = jnp.where(back_usable, back_slot, -1)
    back_rows = select_rows(back_slot, update).reshape(
        seq_count, fsdp_size, slot_count, part_width
    )
    returned = lax.all_to_all(back_rows, "fsdp", split_axis=1, concat_axis=1, tiled=True)
    kept_pos = jnp.arange(kept_most, dtype=jnp.int32)
    their_owner = jnp.mod(my_start[:, None] + kept_pos[None, :], fsdp_size)
    flat_back = their_owner * slot_count + kept_pos[None, :] // fsdp_size
    flat_back = jnp.where(kept_pos[None, :] < my_count[:, None], flat_back, -1)
    landed = select_rows(
        flat_back, returned.reshape(seq_count, fsdp_size * slot_count, part_width)
    )
    valid_pos = jnp.where(kept_pos[None, :] < my_count[:, None], keep_index, -1)
    dense_update = jnp.einsum(
        "skp,skc->spc", onehot(valid_pos, tok_dev), landed, preferred_element_type=jnp.float32
    )
    return tokens.astype(jnp.float32) + dense_update


def solution(mesh):
    placed = (
        P(None, "fsdp", "seq"),
        P(None, "fsdp"),
        P(),
        P(),
        P(),
        P(),
        P("fsdp", "seq"),
        P("fsdp", "seq"),
        P("fsdp", "seq"),
        P("seq", "fsdp"),
    )
    return jax.shard_map(
        shards, mesh=mesh, in_specs=placed, out_specs=P(None, "fsdp", "seq"), check_vma=False
    )
```

```python
import math

import jax
import jax.numpy as jnp
from jax import lax
from jax.sharding import PartitionSpec as P

HD = 128
BLK = 128


epsilon = 1e-05


def onehot(index, size):
    return (index[..., None] == jnp.arange(size, dtype=jnp.int32)).astype(jnp.bfloat16)


def select_rows(index, rows):
    picked = jnp.einsum(
        "skp,spc->skc", onehot(index, rows.shape[1]), rows, preferred_element_type=jnp.float32
    )
    return picked.astype(rows.dtype)


def small_take(table, index):
    hits = index[..., None] == jnp.arange(table.shape[1], dtype=jnp.int32)
    return jnp.sum(jnp.where(hits, table[:, None, :], 0), axis=-1)


def gather_all(x, axis_name, count):
    copies = jnp.broadcast_to(x[None], (count,) + x.shape)
    return lax.all_to_all(copies, axis_name, split_axis=0, concat_axis=0, tiled=True)


def shards(
    tokens, keep_index, keep_count, block_mask, router, norm_gain, w_query, w_key, w_value, w_out
):
    fsdp_size = lax.axis_size("fsdp")
    seq_size = lax.axis_size("seq")
    owner_idx = lax.axis_index("fsdp")
    seq_count, tok_dev, part_width = tokens.shape
    kept_most = keep_index.shape[1]
    slot_count = kept_most // fsdp_size
    own_rows = tok_dev // 8
    block_count = block_mask.shape[1]

    in_rows, q_cols = w_query.shape
    kv_cols = w_key.shape[1]
    qkv_cols = q_cols + 2 * kv_cols
    early_k = w_out.shape[0] // 2
    packed = jnp.concatenate([w_query, w_key, w_value, w_out[:early_k].T], axis=1)
    first = lax.all_gather(packed, "fsdp", axis=0, tiled=True)
    w_qkv = first[:, :qkv_cols]
    w_out_early = first[:, qkv_cols:]
    w_out_late = lax.all_gather(w_out[early_k:].T, "fsdp", axis=0, tiled=True)

    starts = jnp.cumsum(keep_count, axis=1) - keep_count
    range_ends = starts + keep_count
    my_start = lax.dynamic_index_in_dim(starts, owner_idx, 1, keepdims=False)
    my_count = lax.dynamic_index_in_dim(keep_count, owner_idx, 1, keepdims=False)

    owner_ids = jnp.arange(fsdp_size, dtype=jnp.int32)[None, :, None]
    slot_ids = jnp.arange(slot_count, dtype=jnp.int32)[None, None, :]
    first_pick = jnp.mod(owner_ids - my_start[:, None, None], fsdp_size)
    pick_index = (first_pick + slot_ids * fsdp_size).reshape(seq_count, -1)
    usable = pick_index < my_count[:, None]
    src_pos = small_take(keep_index, jnp.minimum(pick_index, kept_most - 1))
    src_pos = jnp.where(usable, src_pos, -1)
    send_rows = select_rows(src_pos, tokens).reshape(seq_count, fsdp_size, slot_count, part_width)
    received = lax.all_to_all(send_rows, "fsdp", split_axis=1, concat_axis=1, tiled=True)

    kept_rank = jnp.arange(own_rows, dtype=jnp.int32) * fsdp_size + owner_idx
    source = jnp.sum((range_ends[:, None, :] <= kept_rank[None, :, None]).astype(jnp.int32), axis=2)
    source_start = small_take(starts, source)
    slot_of = (kept_rank[None, :] - source_start) // fsdp_size
    flat_index = source * slot_count + slot_of
    narrow_rows = select_rows(
        flat_index, received.reshape(seq_count, fsdp_size * slot_count, part_width)
    )
    row_parts = gather_all(narrow_rows, "seq", seq_size)
    full_rows = jnp.transpose(row_parts, (1, 2, 0, 3)).reshape(
        seq_count, own_rows, seq_size * part_width
    )
    full_width = full_rows.shape[2]
    row_total = seq_count * own_rows
    flat_rows = full_rows.reshape(row_total, full_width)
    router_logit = jnp.dot(flat_rows, router, preferred_element_type=jnp.float32)
    gate_value = jax.nn.sigmoid(router_logit)
    wide = flat_rows.astype(jnp.float32)
    mean_square = jnp.mean(wide * wide, axis=1, keepdims=True)
    normed = (wide * lax.rsqrt(mean_square + epsilon) * norm_gain).astype(jnp.bfloat16)
    qkv_sum = jnp.dot(normed, w_qkv, preferred_element_type=jnp.float32).astype(jnp.bfloat16)
    local_kv = kv_cols // HD
    local_heads = q_cols // HD
    group_size = local_heads // local_kv
    queries = qkv_sum[:, :q_cols].reshape(seq_count, own_rows, local_kv, group_size, HD)
    kv_rows = qkv_sum[:, q_cols:].reshape(seq_count, own_rows, 2 * kv_cols)
    kv_parts = gather_all(kv_rows, "fsdp", fsdp_size)
    keep_total = fsdp_size * own_rows
    all_kv = jnp.transpose(kv_parts, (1, 0, 2, 3)).reshape(seq_count, keep_total, 2 * kv_cols)
    key_position = jnp.arange(keep_total, dtype=jnp.int32)
    key_rank = key_position % own_rows * fsdp_size + key_position // own_rows
    block_ids = jnp.arange(block_count, dtype=jnp.int32)
    query_onehot = (kept_rank[:, None] // BLK == block_ids[None, :]).astype(jnp.float32)
    key_onehot = (key_rank[:, None] // BLK == block_ids[None, :]).astype(jnp.float32)
    block_open = jnp.einsum(
        "qa,sab,tb->sqt", query_onehot, block_mask.astype(jnp.float32), key_onehot
    )
    allowed = (block_open > 0.5) & (key_rank[None, None, :] <= kept_rank[None, :, None])
    open_mask = allowed[:, None, None, :, :]
    key_heads = all_kv[:, :, :kv_cols].reshape(seq_count, keep_total, local_kv, HD)
    value_heads = all_kv[:, :, kv_cols:].reshape(seq_count, keep_total, local_kv, HD)
    scores = jnp.einsum(
        "sqkgd,stkd->skgqt", queries, key_heads, preferred_element_type=jnp.float32
    ) * (1.0 / math.sqrt(HD))
    scores = jnp.where(open_mask, scores, jnp.float32(-1e30))
    row_max = jnp.max(scores, axis=4, keepdims=True)
    weights = jnp.where(open_mask, jnp.exp(scores - row_max), jnp.float32(0.0))
    totals = jnp.sum(weights, axis=4, keepdims=True)
    mixed_values = jnp.einsum(
        "skgqt,stkd->sqkgd",
        weights.astype(jnp.bfloat16),
        value_heads,
        preferred_element_type=jnp.float32,
    )
    attended = (
        (mixed_values / jnp.transpose(totals, (0, 3, 1, 2, 4)))
        .astype(jnp.bfloat16)
        .reshape(row_total, local_heads * HD)
    )
    partial_value = jnp.einsum(
        "rk,nk->rn", attended[:, :early_k], w_out_early, preferred_element_type=jnp.float32
    ) + jnp.einsum(
        "rk,nk->rn", attended[:, early_k:], w_out_late, preferred_element_type=jnp.float32
    )
    summed = lax.psum_scatter(
        partial_value.reshape(seq_count, own_rows, full_width).astype(jnp.bfloat16),
        "seq",
        scatter_dimension=2,
        tiled=True,
    ).astype(jnp.float32)
    update = (gate_value.reshape(seq_count, own_rows, 1) * summed).astype(jnp.bfloat16)

    first_back = jnp.mod(owner_idx - starts, fsdp_size)[:, :, None]
    back_pick = first_back + slot_ids * fsdp_size
    back_usable = (back_pick < keep_count[:, :, None]).reshape(seq_count, -1)
    back_slot = ((starts[:, :, None] + back_pick) // fsdp_size).reshape(seq_count, -1)
    back_slot = jnp.where(back_usable, back_slot, -1)
    back_rows = select_rows(back_slot, update).reshape(
        seq_count, fsdp_size, slot_count, part_width
    )
    returned = lax.all_to_all(back_rows, "fsdp", split_axis=1, concat_axis=1, tiled=True)
    kept_pos = jnp.arange(kept_most, dtype=jnp.int32)
    their_owner = jnp.mod(my_start[:, None] + kept_pos[None, :], fsdp_size)
    flat_back = their_owner * slot_count + kept_pos[None, :] // fsdp_size
    flat_back = jnp.where(kept_pos[None, :] < my_count[:, None], flat_back, -1)
    landed = select_rows(
        flat_back, returned.reshape(seq_count, fsdp_size * slot_count, part_width)
    )
    valid_pos = jnp.where(kept_pos[None, :] < my_count[:, None], keep_index, -1)
    dense_update = jnp.einsum(
        "skp,skc->spc", onehot(valid_pos, tok_dev), landed, preferred_element_type=jnp.float32
    )
    return tokens.astype(jnp.float32) + dense_update


def solution(mesh):
    placed = (
        P(None, "fsdp", "seq"),
        P(None, "fsdp"),
        P(),
        P(),
        P(),
        P(),
        P("fsdp", "seq"),
        P("fsdp", "seq"),
        P("fsdp", "seq"),
        P("seq", "fsdp"),
    )
    return jax.shard_map(
        shards, mesh=mesh, in_specs=placed, out_specs=P(None, "fsdp", "seq"), check_vma=False
    )
```

```python
import math

import jax
import jax.numpy as jnp
from jax import lax
from jax.sharding import PartitionSpec as P

HD = 128
BLK = 128


epsilon = 1e-05


def onehot(index, size):
    return (index[..., None] == jnp.arange(size, dtype=jnp.int32)).astype(jnp.bfloat16)


def select_rows(index, rows):
    picked = jnp.einsum(
        "skp,spc->skc", onehot(index, rows.shape[1]), rows, preferred_element_type=jnp.float32
    )
    return picked.astype(rows.dtype)


def small_take(table, index):
    hits = index[..., None] == jnp.arange(table.shape[1], dtype=jnp.int32)
    return jnp.sum(jnp.where(hits, table[:, None, :], 0), axis=-1)


def gather_all(x, axis_name, count):
    copies = jnp.broadcast_to(x[None], (count,) + x.shape)
    return lax.all_to_all(copies, axis_name, split_axis=0, concat_axis=0, tiled=True)


def shards(
    tokens, keep_index, keep_count, block_mask, router, norm_gain, w_query, w_key, w_value, w_out
):
    fsdp_size = lax.axis_size("fsdp")
    seq_size = lax.axis_size("seq")
    owner_idx = lax.axis_index("fsdp")
    seq_count, tok_dev, part_width = tokens.shape
    kept_most = keep_index.shape[1]
    slot_count = kept_most // fsdp_size
    own_rows = tok_dev // 8
    block_count = block_mask.shape[1]

    in_rows, q_cols = w_query.shape
    kv_cols = w_key.shape[1]
    qkv_cols = q_cols + 2 * kv_cols
    packed = jnp.zeros((in_rows, qkv_cols), w_query.dtype)
    packed = lax.dynamic_update_slice(packed, w_query, (0, 0))
    packed = lax.dynamic_update_slice(packed, w_key, (0, q_cols))
    packed = lax.dynamic_update_slice(packed, w_value, (0, q_cols + kv_cols))
    w_qkv = lax.all_gather(packed, "fsdp", axis=0, tiled=True)
    w_out_t = lax.all_gather(w_out.T, "fsdp", axis=0, tiled=True)

    starts = jnp.cumsum(keep_count, axis=1) - keep_count
    range_ends = starts + keep_count
    my_start = lax.dynamic_index_in_dim(starts, owner_idx, 1, keepdims=False)
    my_count = lax.dynamic_index_in_dim(keep_count, owner_idx, 1, keepdims=False)

    owner_ids = jnp.arange(fsdp_size, dtype=jnp.int32)[None, :, None]
    slot_ids = jnp.arange(slot_count, dtype=jnp.int32)[None, None, :]
    first_pick = jnp.mod(owner_ids - my_start[:, None, None], fsdp_size)
    pick_index = (first_pick + slot_ids * fsdp_size).reshape(seq_count, -1)
    usable = pick_index < my_count[:, None]
    src_pos = small_take(keep_index, jnp.minimum(pick_index, kept_most - 1))
    src_pos = jnp.where(usable, src_pos, -1)
    send_rows = select_rows(src_pos, tokens).reshape(seq_count, fsdp_size, slot_count, part_width)
    received = lax.all_to_all(send_rows, "fsdp", split_axis=1, concat_axis=1, tiled=True)

    kept_rank = jnp.arange(own_rows, dtype=jnp.int32) * fsdp_size + owner_idx
    source = jnp.sum((range_ends[:, None, :] <= kept_rank[None, :, None]).astype(jnp.int32), axis=2)
    source_start = small_take(starts, source)
    slot_of = (kept_rank[None, :] - source_start) // fsdp_size
    flat_index = source * slot_count + slot_of
    narrow_rows = select_rows(
        flat_index, received.reshape(seq_count, fsdp_size * slot_count, part_width)
    )
    row_parts = gather_all(narrow_rows, "seq", seq_size)
    full_rows = jnp.transpose(row_parts, (1, 2, 0, 3)).reshape(
        seq_count, own_rows, seq_size * part_width
    )
    full_width = full_rows.shape[2]
    row_total = seq_count * own_rows
    flat_rows = full_rows.reshape(row_total, full_width)
    router_logit = jnp.dot(flat_rows, router, preferred_element_type=jnp.float32)
    gate_value = jax.nn.sigmoid(router_logit)
    wide = flat_rows.astype(jnp.float32)
    mean_square = jnp.mean(wide * wide, axis=1, keepdims=True)
    normed = (wide * lax.rsqrt(mean_square + epsilon) * norm_gain).astype(jnp.bfloat16)
    qkv_sum = jnp.dot(normed, w_qkv, preferred_element_type=jnp.float32).astype(jnp.bfloat16)
    local_kv = kv_cols // HD
    local_heads = q_cols // HD
    group_size = local_heads // local_kv
    queries = qkv_sum[:, :q_cols].reshape(seq_count, own_rows, local_kv, group_size, HD)
    kv_rows = qkv_sum[:, q_cols:].reshape(seq_count, own_rows, 2 * kv_cols)
    kv_parts = gather_all(kv_rows, "fsdp", fsdp_size)
    keep_total = fsdp_size * own_rows
    all_kv = jnp.transpose(kv_parts, (1, 0, 2, 3)).reshape(seq_count, keep_total, 2 * kv_cols)
    key_position = jnp.arange(keep_total, dtype=jnp.int32)
    key_rank = key_position % own_rows * fsdp_size + key_position // own_rows
    block_ids = jnp.arange(block_count, dtype=jnp.int32)
    query_onehot = (kept_rank[:, None] // BLK == block_ids[None, :]).astype(jnp.float32)
    key_onehot = (key_rank[:, None] // BLK == block_ids[None, :]).astype(jnp.float32)
    block_open = jnp.einsum(
        "qa,sab,tb->sqt", query_onehot, block_mask.astype(jnp.float32), key_onehot
    )
    allowed = (block_open > 0.5) & (key_rank[None, None, :] <= kept_rank[None, :, None])
    open_mask = allowed[:, None, None, :, :]
    key_heads = all_kv[:, :, :kv_cols].reshape(seq_count, keep_total, local_kv, HD)
    value_heads = all_kv[:, :, kv_cols:].reshape(seq_count, keep_total, local_kv, HD)
    scores = jnp.einsum(
        "sqkgd,stkd->skgqt", queries, key_heads, preferred_element_type=jnp.float32
    ) * (1.0 / math.sqrt(HD))
    scores = jnp.where(open_mask, scores, jnp.float32(-1e30))
    row_max = jnp.max(scores, axis=4, keepdims=True)
    weights = jnp.where(open_mask, jnp.exp(scores - row_max), jnp.float32(0.0))
    totals = jnp.sum(weights, axis=4, keepdims=True)
    mixed_values = jnp.einsum(
        "skgqt,stkd->sqkgd",
        weights.astype(jnp.bfloat16),
        value_heads,
        preferred_element_type=jnp.float32,
    )
    attended = (
        (mixed_values / jnp.transpose(totals, (0, 3, 1, 2, 4)))
        .astype(jnp.bfloat16)
        .reshape(row_total, local_heads * HD)
    )
    partial_value = jnp.einsum(
        "rk,nk->rn", attended, w_out_t, preferred_element_type=jnp.float32
    )
    summed = lax.psum_scatter(
        partial_value.reshape(seq_count, own_rows, full_width).astype(jnp.bfloat16),
        "seq",
        scatter_dimension=2,
        tiled=True,
    ).astype(jnp.float32)
    update = (gate_value.reshape(seq_count, own_rows, 1) * summed).astype(jnp.bfloat16)

    first_back = jnp.mod(owner_idx - starts, fsdp_size)[:, :, None]
    back_pick = first_back + slot_ids * fsdp_size
    back_usable = (back_pick < keep_count[:, :, None]).reshape(seq_count, -1)
    back_slot = ((starts[:, :, None] + back_pick) // fsdp_size).reshape(seq_count, -1)
    back_slot = jnp.where(back_usable, back_slot, -1)
    back_rows = select_rows(back_slot, update).reshape(
        seq_count, fsdp_size, slot_count, part_width
    )
    returned = lax.all_to_all(back_rows, "fsdp", split_axis=1, concat_axis=1, tiled=True)
    kept_pos = jnp.arange(kept_most, dtype=jnp.int32)
    their_owner = jnp.mod(my_start[:, None] + kept_pos[None, :], fsdp_size)
    flat_back = their_owner * slot_count + kept_pos[None, :] // fsdp_size
    flat_back = jnp.where(kept_pos[None, :] < my_count[:, None], flat_back, -1)
    landed = select_rows(
        flat_back, returned.reshape(seq_count, fsdp_size * slot_count, part_width)
    )
    valid_pos = jnp.where(kept_pos[None, :] < my_count[:, None], keep_index, -1)
    dense_update = jnp.einsum(
        "skp,skc->spc", onehot(valid_pos, tok_dev), landed, preferred_element_type=jnp.float32
    )
    return tokens.astype(jnp.float32) + dense_update


def solution(mesh):
    placed = (
        P(None, "fsdp", "seq"),
        P(None, "fsdp"),
        P(),
        P(),
        P(),
        P(),
        P("fsdp", "seq"),
        P("fsdp", "seq"),
        P("fsdp", "seq"),
        P("seq", "fsdp"),
    )
    return jax.shard_map(
        shards, mesh=mesh, in_specs=placed, out_specs=P(None, "fsdp", "seq"), check_vma=False
    )
```
